128 devices in a mesh: pairs: 32 (over y, z, core), coup: 4 (over x).
Axes of the slice: x: 4, y: 4, z: 4, core: 2. Of those that a mesh axis runs over, the one named last changes fastest.
Arguments:
- coupling_list: int32 [3, 2048], P(None, 'pairs'), may hold values from 0 to 511, as said below
- pair_slot: int32 [128], replicated, may hold values from 0 to 127, as said below
- coupling_weight: float32 [2048], P('pairs'), may hold values from -1 to 1
- integrals: bfloat16 [128, 448, 448], P(('pairs', 'coup')), may hold values from -6 to 6
- orbital_energy: float32 [128, 448], P(('pairs', 'coup')), may hold values from 0.5 to 3
- pair_energy: float32 [128], P(('pairs', 'coup')), may hold values from 0.3 to 3
- intersections: bfloat16 [512, 448, 448], P(('pairs', 'coup')), may hold values from -0.25 to 0.25
Outputs:
- amplitudes: float32 [128, 448, 448], P(('pairs', 'coup'))
The draws below stay inside these ranges and needn't reach their ends.
Inputs may be any that keep to these rules, and one draw needn't show every extreme that they name: `coupling_list`: row 0 and row 1 hold pair numbers, row 2 an intersection index. Positions g * 64 to (g + 1) * 64 - 1 form block g: its pairs i have rows (pair_slot) in g * 4 to (g + 1) * 4 - 1 and its intersection indices lie in g * 16 to (g + 1) * 16 - 1; for every h, exactly two couplings of block g have pair j with its row in h * 4 to (h + 1) * 4 - 1, and both name the same pair j. In each block at most 32 couplings have pair i with its row in the same 1 row of one device, and exactly 32 do for one such device. Likewise in each block at most 32 couplings have an intersection index among the same 4 indices of one device, and exactly 32 do for one such device. `pair_slot`: A permutation of the pairs.
All inputs are finite; a program needn't handle non-finite values.
Results may differ from the reference program's by a relative error of at most 0.0024.
Values may be sent and summed in bfloat16 or wider, within the bound.
No kernel may reach another device: no remote copies, remote signals or barrier semaphores. Data moves between devices by JAX's collectives and lax.ppermute only.
A program may use at most 128 MiB of HBM per device.

```python
import math
from functools import partial
import jax
import jax.numpy as jnp
from jax import lax

NV = 448
PAIR_DEV = 1
OV_DEV = 4
ITERS = 2
TOTAL_PAIRS = 128
GROUP_PAIRS = 4
TOTAL_INTERSECTIONS = 512
GROUP_INTERSECTIONS = 16
GROUP_COUPLINGS = 64
TOTAL_COUPLINGS = 2048
HCAP = 32
N_PAIRS = 32
N_COUP = 4


def slot_table(key):
    return jax.random.permutation(jax.random.fold_in(key, 11), TOTAL_PAIRS).astype(jnp.int32)


def draw_pair_slot(key, part):
    return slot_table(key)


def capped_members(key, rank_salt, busy_salt):
    shuffler = jax.vmap(partial(jax.random.permutation, x=GROUP_COUPLINGS))
    load_rank = shuffler(jax.random.split(jax.random.fold_in(key, rank_salt), N_PAIRS)).astype(jnp.int32)
    busiest = jax.random.randint(jax.random.fold_in(key, busy_salt), (N_PAIRS, 1), 0, N_COUP)
    spare = (busiest + 1 + (load_rank - HCAP) % (N_COUP - 1)) % N_COUP
    return jnp.where(load_rank < HCAP, busiest, spare)


def draw_coupling_list(key, part):
    slot_of_pair = slot_table(key)
    pair_of_row = jnp.argsort(slot_of_pair).astype(jnp.int32)
    group_ids = jnp.arange(N_PAIRS, dtype=jnp.int32)[:, None]
    shuffler = jax.vmap(partial(jax.random.permutation, x=GROUP_COUPLINGS))
    read_rank = shuffler(jax.random.split(jax.random.fold_in(key, 21), N_PAIRS)).astype(jnp.int32)
    source_group = read_rank // 2
    read_pick = jax.random.randint(jax.random.fold_in(key, 22), (N_PAIRS, N_PAIRS), 0, GROUP_PAIRS)
    read_row = source_group * GROUP_PAIRS + jnp.take_along_axis(read_pick, source_group, axis=1)
    owner_member = capped_members(key, 23, 24)
    within = jax.random.randint(jax.random.fold_in(key, 25), (N_PAIRS, GROUP_COUPLINGS), 0, PAIR_DEV)
    owner_row = group_ids * GROUP_PAIRS + owner_member * PAIR_DEV + within
    intersection_member = capped_members(key, 27, 28)
    intersection_within = jax.random.randint(jax.random.fold_in(key, 26), (N_PAIRS, GROUP_COUPLINGS), 0, OV_DEV)
    intersection_index = group_ids * GROUP_INTERSECTIONS + intersection_member * OV_DEV + intersection_within
    pair_first = pair_of_row[owner_row.reshape(-1)]
    pair_second = pair_of_row[read_row.reshape(-1)]
    return jnp.stack([pair_first, pair_second, intersection_index.reshape(-1)]).astype(jnp.int32)


def block_levels(rng, shape, cuts, least, high):
    def one(axis_at, shards_of):
        draws = jax.random.uniform(jax.random.fold_in(jax.random.fold_in(rng, 6), axis_at), (shards_of,), jnp.float32, least / len(cuts), high / len(cuts))
        return jnp.repeat(jnp.exp(draws), shape[axis_at] // shards_of).reshape((-1,) + (1,) * (len(shape) - axis_at - 1))

    gain = one(*cuts[0])
    for cut in cuts[1:]:
        gain = gain * one(*cut)
    return gain


def centred(stream_key, extent, width, bound, pieces=(), held_as=jnp.bfloat16):
    result = jax.random.normal(stream_key, extent, jnp.float32) * width
    if len(pieces) > 0:
        result = block_levels(stream_key, extent, pieces, -0.22, 0.18) * result
    return jnp.clip(result, min=-bound, max=bound).astype(held_as)


def setup_inputs(seed: int = 0) -> dict:
    arg_keys = jax.random.split(jax.random.key(seed), 8)
    return {
        "coupling_list": draw_coupling_list(jax.random.fold_in(arg_keys[7], 71), 0),
        "pair_slot": draw_pair_slot(jax.random.fold_in(arg_keys[7], 71), 0),
        "coupling_weight": jnp.clip(jax.random.uniform(arg_keys[2], (TOTAL_COUPLINGS,), jnp.float32, -1.0, 1.0) * block_levels(arg_keys[2], (TOTAL_COUPLINGS,), ((0, 32),), -0.4, 0.0), -1.0, 1.0),
        "integrals": centred(arg_keys[3], (TOTAL_PAIRS, NV, NV), 1.0, 6.0, ((0, 128),)),
        "orbital_energy": jnp.clip(0.5 + 2.5 * jax.random.uniform(arg_keys[4], (TOTAL_PAIRS, NV), jnp.float32) ** block_levels(arg_keys[4], (TOTAL_PAIRS, NV), ((0, 128),), -0.2, 0.2), 0.5, 3.0),
        "pair_energy": jnp.clip(jnp.exp(math.log(3.0) - 2.3025851 * jax.random.uniform(arg_keys[5], (TOTAL_PAIRS,), jnp.float32) ** block_levels(arg_keys[5], (TOTAL_PAIRS,), ((0, 128),), -0.2, 0.2)), 0.3, 3.0),
        "intersections": centred(arg_keys[6], (TOTAL_INTERSECTIONS, NV, NV), NV ** -0.5, 0.25, ((0, 128),)),
    }


def reference(coupling_list, pair_slot, coupling_weight, integrals, orbital_energy, pair_energy, intersections):
    owner_row = pair_slot[coupling_list[0]].astype(jnp.int32)
    reader_row = pair_slot[coupling_list[1]].astype(jnp.int32)
    intersection_index = coupling_list[2].astype(jnp.int32)
    denominator = orbital_energy[:, :, None] + orbital_energy[:, None, :] + pair_energy[:, None, None]
    integral_f = integrals.astype(jnp.float32)
    amplitudes = -integral_f / denominator
    total = coupling_list.shape[1]
    block_size = math.gcd(total, 64)
    for iteration in range(ITERS):
        rounded = amplitudes.astype(jnp.bfloat16)

        def accumulate(block_turn, coupled):
            first_slot = (block_turn * block_size).astype(jnp.int32)
            read_block = lax.dynamic_slice_in_dim(reader_row, first_slot, block_size)
            owner_block = lax.dynamic_slice_in_dim(owner_row, first_slot, block_size)
            intersection_block = lax.dynamic_slice_in_dim(intersection_index, first_slot, block_size)
            weight_block = lax.dynamic_slice_in_dim(coupling_weight, first_slot, block_size)
            amp_block = rounded[read_block].astype(jnp.float32)
            ovl_block = intersections[intersection_block].astype(jnp.float32)
            left_product = jnp.einsum("sab,sbc->sac", ovl_block, amp_block).astype(jnp.bfloat16)
            left_product = lax.optimization_barrier(left_product).astype(jnp.float32)
            full_product = jnp.einsum("sac,sdc->sad", left_product, ovl_block)
            return coupled.at[owner_block].add(weight_block[:, None, None] * full_product)

        coupled = lax.fori_loop(0, total // block_size, accumulate, jnp.zeros(amplitudes.shape, jnp.float32))
        amplitudes = -(integral_f + coupled) / denominator
    return amplitudes
```

```python
import functools

import jax
import jax.numpy as jnp
from jax import lax
from jax.experimental import pallas as pl
from jax.experimental.pallas import tpu as pltpu
from jax.sharding import Mesh
from jax.sharding import PartitionSpec as P


ITERS = 2
PAIRS = ("pairs_0", "pairs_1", "pairs_2")
PAIRS_COUP = ("pairs_0", "pairs_1", "pairs_2", "coup")


def lookup(lookup_table, queries):
    columns = lax.broadcasted_iota(jnp.int32, (queries.shape[0], lookup_table.shape[0]), 1)
    return jnp.sum(jnp.where(queries[:, None] == columns, lookup_table[None, :], 0), axis=1)


def shift(x, step):
    peers = lax.axis_size("coup")
    return lax.ppermute(x, "coup", [(i, (i + step) % peers) for i in range(peers)])


def exchange_wanted(wanted_here):
    tiles = wanted_here.reshape(16, 2, 1)
    tiles = lax.all_to_all(tiles, "pairs_2", 1, 1, tiled=True)
    tiles = lax.all_to_all(tiles, ("pairs_0", "pairs_1"), 0, 0, tiled=True)
    return tiles.reshape(32)


def couple_kernel(
    slices, sched, weights, t_hbm, o_own, o_next, o_far_a, o_far_b, o_last, kept, out_1, out_2, out_3,
    acc, t_buf, o_buf, even_0, even_1, odd_0, odd_1, t_sems, o_sems,
):
    sources, strip = t_buf.shape[0], t_buf.shape[1]
    count = 2 * sources
    offset = pl.multiple_of(sched[2 * count], 16)
    lane = pl.multiple_of(sched[2 * count + 1], 128)
    member = sched[2 * count + 2]
    copies, first = [], 0
    for i, piece in enumerate((o_own, o_next, o_far_a, o_far_b, o_last)):
        size = piece.shape[0]
        copies.append(pltpu.make_async_copy(piece, o_buf.at[pl.ds(first, size)], o_sems.at[i]))
        first += size
    copies.append(pltpu.make_async_copy(t_hbm, t_buf, t_sems.at[0]))
    for copy in copies:
        copy.start()
    for ref in (acc, even_0, even_1, odd_0, odd_1):
        ref[...] = jnp.zeros_like(ref)
    for copy in copies:
        copy.wait()

    def right(h, s, ref):
        product = lax.dot_general(
            t_buf[h], o_buf[sched[2 * h + s]], (((1,), (1,)), ((), ())), preferred_element_type=jnp.float32
        )
        ref[pl.ds(offset, strip), :] = product.astype(jnp.bfloat16)

    def left(h, s, ref):
        k = 2 * h + s
        product = jnp.dot(
            o_buf[sched[k], :, pl.ds(lane, 256)], ref[...], preferred_element_type=jnp.float32
        )
        acc[sched[count + k]] += weights[k] * product

    right(0, 0, even_0)
    right(0, 1, even_1)

    def step(i, carry):
        h = 2 * i
        right(h + 1, 0, odd_0)
        left(h, 0, even_0)
        right(h + 1, 1, odd_1)
        left(h, 1, even_1)
        after = jnp.minimum(h + 2, sources - 1)
        right(after, 0, even_0)
        left(h + 1, 0, odd_0)
        right(after, 1, even_1)
        left(h + 1, 1, odd_1)
        return carry

    lax.fori_loop(0, sources // 2, step, 0)
    members = acc.shape[0]
    for d, out in enumerate((kept, out_1, out_2, out_3)):
        peer = lax.rem(member + d, members)
        if slices:
            rows = pl.ds(pl.multiple_of(peer * strip, 16), strip)
            for r in range(members):
                out[r] = acc[lax.rem(peer + r, members), rows, :].astype(out.dtype)
        else:
            out[...] = acc[peer].astype(out.dtype)


def couple(sched, weights, strips, pieces, coup, slices):
    _, strip, lanes = strips.shape
    width = pieces[0].shape[1]
    part = (coup, strip, width) if slices else (width, width)
    total = sum(piece.shape[0] for piece in pieces)
    whole = pl.BlockSpec(part, lambda i, *_: (0,) * len(part))
    half = pltpu.VMEM((256, width), jnp.bfloat16)
    return pl.pallas_call(
        functools.partial(couple_kernel, slices),
        out_shape=[jax.ShapeDtypeStruct(part, jnp.float32)] + [jax.ShapeDtypeStruct(part, jnp.bfloat16)] * 3,
        grid_spec=pltpu.PrefetchScalarGridSpec(
            num_scalar_prefetch=2,
            grid=(1,),
            in_specs=[pl.BlockSpec(memory_space=pl.ANY)] * (1 + len(pieces)),
            out_specs=[whole] * 4,
            scratch_shapes=[
                pltpu.VMEM((coup, width, width), jnp.float32),
                pltpu.VMEM(strips.shape, jnp.bfloat16),
                pltpu.VMEM((total, width, lanes), jnp.bfloat16),
                half, half, half, half,
                pltpu.SemaphoreType.DMA((1,)),
                pltpu.SemaphoreType.DMA((len(pieces),)),
            ],
        ),
        compiler_params=pltpu.CompilerParams(vmem_limit_bytes=60 * 2**20),
        name="couple_strips" if slices else "couple_pairs",
    )(sched, weights, strips, *pieces)


def sum_parts(kept, parts):
    for d, part in enumerate(parts):
        kept = kept + shift(part, d + 1).astype(jnp.float32)
    return kept


def amplitudes_of(
    coupling_list, pair_slot, coupling_weight, integrals, orbital_energy, pair_energy, intersections
):
    groups = lax.axis_size(PAIRS)
    coup = lax.axis_size("coup")
    group_index = lax.axis_index(PAIRS)
    member = lax.axis_index("coup")
    ov_dev, width = intersections.shape[0], integrals.shape[-1]
    count = coupling_list.shape[1]
    strip = width // coup
    lanes = -width % 128

    padded = jnp.pad(intersections, ((0, 0), (0, 0), (0, lanes)))
    half = ov_dev // 2
    o_next, o_last = shift(padded, -1), shift(padded, 1)
    far_a, far_b = shift(o_last[:half], 1), shift(o_next[half:], -1)
    pieces = (padded, o_next, far_a, far_b, o_last)

    owner_row = lookup(pair_slot, coupling_list[0]) - group_index * coup
    reader_row = lookup(pair_slot, coupling_list[1])
    source, read_pair = reader_row // coup, reader_row % coup
    local_o = coupling_list[2] - group_index * (ov_dev * coup)
    local_o = (local_o - member * ov_dev) % (ov_dev * coup)
    position = lax.iota(jnp.int32, count)
    twin = jnp.max(
        jnp.where((source[None, :] == source[:, None]) & (position[None, :] < position[:, None]), 1, 0), axis=1
    )
    slot = 2 * source + twin
    chosen = slot[None, :] == position[:, None]
    pick = lambda v: jnp.sum(jnp.where(chosen, v[None, :], jnp.zeros((), v.dtype)), axis=1)
    strip_row = member * strip
    lane_tile = jnp.minimum(strip_row // 128, 2) * 128
    sched = jnp.concatenate(
        [pick(local_o), pick(owner_row), jnp.stack([strip_row - lane_tile, lane_tile, member])]
    ).astype(jnp.int32)
    weights = pick(coupling_weight)
    asked = source[None, :] == lax.broadcasted_iota(jnp.int32, (groups, count), 0)
    wanted = exchange_wanted(jnp.max(jnp.where(asked, read_pair[None, :], 0), axis=1))

    flipped = jnp.pad(jnp.transpose(integrals[0]), ((0, 0), (0, lanes)))
    rows_of = lambda d: lax.dynamic_slice_in_dim(flipped, lax.rem(member + d, coup) * strip, strip)
    sent = [shift(rows_of(coup - e), coup - e) for e in range(1, coup)]
    integral_strips = jnp.stack([rows_of(0)] + sent)
    energies = jnp.concatenate([orbital_energy[0], pair_energy])[None]
    energies = jnp.concatenate([energies] + [shift(energies, -e) for e in range(1, coup)])
    orbital, pair = energies[:, :width], energies[:, width]
    own_rows = lax.dynamic_slice_in_dim(orbital, strip_row, strip, axis=1)
    all_columns = jnp.pad(orbital, ((0, 0), (0, lanes)))
    strip_denominator = own_rows[:, :, None] + all_columns[:, None, :] + pair[:, None, None]
    integral_f = integral_strips.astype(jnp.float32)
    amplitudes = -integral_f / strip_denominator
    wanted = (wanted - member) % coup

    for iteration in range(ITERS):
        rounded = amplitudes.astype(jnp.bfloat16)
        outgoing = rounded.at[wanted].get(mode="promise_in_bounds")
        arrived = lax.all_to_all(outgoing, PAIRS, 0, 0, tiled=True)
        last = iteration == ITERS - 1
        kept, *parts = couple(sched, weights, arrived, pieces, coup, not last)
        coupled = sum_parts(kept, parts)
        if not last:
            coupled = jnp.pad(coupled, ((0, 0), (0, 0), (0, lanes)))
            amplitudes = -(integral_f + coupled) / strip_denominator
    denominator = orbital_energy[:, :, None] + orbital_energy[:, None, :] + pair_energy[:, None, None]
    return -(integrals.astype(jnp.float32) + jnp.transpose(coupled)[None]) / denominator


def solution(mesh):
    split = Mesh(
        mesh.devices.reshape(4, 4, 2, mesh.shape["coup"]), ("pairs_0", "pairs_1", "pairs_2", "coup")
    )
    in_specs = (
        P(None, PAIRS),
        P(),
        P(PAIRS),
        P(PAIRS_COUP, None, None),
        P(PAIRS_COUP, None),
        P(PAIRS_COUP),
        P(PAIRS_COUP, None, None),
    )
    return jax.shard_map(
        amplitudes_of, mesh=split, in_specs=in_specs, out_specs=P(PAIRS_COUP, None, None), check_vma=False
    )
```

```python
import functools

import jax
import jax.numpy as jnp
from jax import lax
from jax.experimental import pallas as pl
from jax.experimental.pallas import tpu as pltpu
from jax.sharding import Mesh
from jax.sharding import PartitionSpec as P


ITERS = 2
PAIRS = ("pairs_0", "pairs_1", "pairs_2")
PAIRS_COUP = ("pairs_0", "pairs_1", "pairs_2", "coup")


def lookup(lookup_table, queries):
    columns = lax.broadcasted_iota(jnp.int32, (queries.shape[0], lookup_table.shape[0]), 1)
    return jnp.sum(jnp.where(queries[:, None] == columns, lookup_table[None, :], 0), axis=1)


def shift(x, step):
    peers = lax.axis_size("coup")
    return lax.ppermute(x, "coup", [(i, (i + step) % peers) for i in range(peers)])


def exchange_wanted(wanted_here):
    tiles = wanted_here.reshape(16, 2, 1)
    tiles = lax.all_to_all(tiles, "pairs_2", 1, 1, tiled=True)
    tiles = lax.all_to_all(tiles, ("pairs_0", "pairs_1"), 0, 0, tiled=True)
    return tiles.reshape(32)


def couple_kernel(
    slices, sched, weights, t_hbm, o_own, o_1, o_2, o_3, o_4, o_5, o_6, kept, out_1, out_2, out_3,
    acc, t_buf, o_buf, even_0, even_1, odd_0, odd_1, t_sems, o_sems,
):
    sources, strip = t_buf.shape[0], t_buf.shape[1]
    count = 2 * sources
    offset = pl.multiple_of(sched[2 * count], 16)
    lane = pl.multiple_of(sched[2 * count + 1], 128)
    member = sched[2 * count + 2]
    copies, first = [], 0
    for i, piece in enumerate((o_own, o_1, o_2, o_3, o_4, o_5, o_6)):
        size = piece.shape[0]
        copies.append(pltpu.make_async_copy(piece, o_buf.at[pl.ds(first, size)], o_sems.at[i]))
        first += size
    copies.append(pltpu.make_async_copy(t_hbm, t_buf, t_sems.at[0]))
    for copy in copies:
        copy.start()
    for ref in (acc, even_0, even_1, odd_0, odd_1):
        ref[...] = jnp.zeros_like(ref)
    for copy in copies:
        copy.wait()

    def right(h, s, ref):
        product = lax.dot_general(
            t_buf[h], o_buf[sched[2 * h + s]], (((1,), (1,)), ((), ())), preferred_element_type=jnp.float32
        )
        ref[pl.ds(offset, strip), :] = product.astype(jnp.bfloat16)

    def left(h, s, ref):
        k = 2 * h + s
        product = jnp.dot(
            o_buf[sched[k], :, pl.ds(lane, 256)], ref[...], preferred_element_type=jnp.float32
        )
        acc[sched[count + k]] += weights[k] * product

    right(0, 0, even_0)
    right(0, 1, even_1)

    def step(i, carry):
        h = 2 * i
        right(h + 1, 0, odd_0)
        left(h, 0, even_0)
        right(h + 1, 1, odd_1)
        left(h, 1, even_1)
        after = jnp.minimum(h + 2, sources - 1)
        right(after, 0, even_0)
        left(h + 1, 0, odd_0)
        right(after, 1, even_1)
        left(h + 1, 1, odd_1)
        return carry

    lax.fori_loop(0, sources // 2, step, 0)
    members = acc.shape[0]
    for d, out in enumerate((kept, out_1, out_2, out_3)):
        peer = lax.rem(member + d, members)
        if slices:
            rows = pl.ds(pl.multiple_of(peer * strip, 16), strip)
            for r in range(members):
                out[r] = acc[lax.rem(peer + r, members), rows, :].astype(out.dtype)
        else:
            out[...] = acc[peer].astype(out.dtype)


def couple(sched, weights, strips, pieces, coup, slices):
    _, strip, lanes = strips.shape
    width = pieces[0].shape[1]
    part = (coup, strip, width) if slices else (width, width)
    total = sum(piece.shape[0] for piece in pieces)
    whole = pl.BlockSpec(part, lambda i, *_: (0,) * len(part))
    half = pltpu.VMEM((256, width), jnp.bfloat16)
    return pl.pallas_call(
        functools.partial(couple_kernel, slices),
        out_shape=[jax.ShapeDtypeStruct(part, jnp.float32)] + [jax.ShapeDtypeStruct(part, jnp.bfloat16)] * 3,
        grid_spec=pltpu.PrefetchScalarGridSpec(
            num_scalar_prefetch=2,
            grid=(1,),
            in_specs=[pl.BlockSpec(memory_space=pl.ANY)] * (1 + len(pieces)),
            out_specs=[whole] * 4,
            scratch_shapes=[
                pltpu.VMEM((coup, width, width), jnp.float32),
                pltpu.VMEM(strips.shape, jnp.bfloat16),
                pltpu.VMEM((total, width, lanes), jnp.bfloat16),
                half, half, half, half,
                pltpu.SemaphoreType.DMA((1,)),
                pltpu.SemaphoreType.DMA((len(pieces),)),
            ],
        ),
        compiler_params=pltpu.CompilerParams(vmem_limit_bytes=60 * 2**20),
        name="couple_strips" if slices else "couple_pairs",
    )(sched, weights, strips, *pieces)


def sum_parts(kept, parts):
    for d, part in enumerate(parts):
        kept = kept + shift(part, d + 1).astype(jnp.float32)
    return kept


def amplitudes_of(
    coupling_list, pair_slot, coupling_weight, integrals, orbital_energy, pair_energy, intersections
):
    groups = lax.axis_size(PAIRS)
    coup = lax.axis_size("coup")
    group_index = lax.axis_index(PAIRS)
    member = lax.axis_index("coup")
    ov_dev, width = intersections.shape[0], integrals.shape[-1]
    count = coupling_list.shape[1]
    strip = width // coup
    lanes = -width % 128

    half = ov_dev // 2
    padded = jnp.pad(intersections, ((0, 0), (0, 0), (0, lanes)))
    low, high = padded[:half], padded[half:]
    last_low, next_high = shift(low, 1), shift(high, -1)
    last_high, next_low = shift(high, 1), shift(low, -1)
    far_low, far_high = shift(last_low, 1), shift(next_high, -1)
    pieces = (padded, next_low, next_high, far_low, far_high, last_low, last_high)

    owner_row = lookup(pair_slot, coupling_list[0]) - group_index * coup
    reader_row = lookup(pair_slot, coupling_list[1])
    source, read_pair = reader_row // coup, reader_row % coup
    local_o = coupling_list[2] - group_index * (ov_dev * coup)
    local_o = (local_o - member * ov_dev) % (ov_dev * coup)
    position = lax.iota(jnp.int32, count)
    twin = jnp.max(
        jnp.where((source[None, :] == source[:, None]) & (position[None, :] < position[:, None]), 1, 0), axis=1
    )
    slot = 2 * source + twin
    chosen = slot[None, :] == position[:, None]
    pick = lambda v: jnp.sum(jnp.where(chosen, v[None, :], jnp.zeros((), v.dtype)), axis=1)
    strip_row = member * strip
    lane_tile = jnp.minimum(strip_row // 128, 2) * 128
    sched = jnp.concatenate(
        [pick(local_o), pick(owner_row), jnp.stack([strip_row - lane_tile, lane_tile, member])]
    ).astype(jnp.int32)
    weights = pick(coupling_weight)
    asked = source[None, :] == lax.broadcasted_iota(jnp.int32, (groups, count), 0)
    wanted = exchange_wanted(jnp.max(jnp.where(asked, read_pair[None, :], 0), axis=1))

    flipped = jnp.pad(jnp.transpose(integrals[0]), ((0, 0), (0, lanes)))
    rows_of = lambda d: lax.dynamic_slice_in_dim(flipped, lax.rem(member + d, coup) * strip, strip)
    sent = [shift(rows_of(coup - e), coup - e) for e in range(1, coup)]
    integral_strips = jnp.stack([rows_of(0)] + sent)
    energies = jnp.concatenate([orbital_energy[0], pair_energy])[None]
    energies = jnp.concatenate([energies] + [shift(energies, -e) for e in range(1, coup)])
    orbital, pair = energies[:, :width], energies[:, width]
    own_rows = lax.dynamic_slice_in_dim(orbital, strip_row, strip, axis=1)
    all_columns = jnp.pad(orbital, ((0, 0), (0, lanes)))
    strip_denominator = own_rows[:, :, None] + all_columns[:, None, :] + pair[:, None, None]
    integral_f = integral_strips.astype(jnp.float32)
    amplitudes = -integral_f / strip_denominator
    wanted = (wanted - member) % coup

    for iteration in range(ITERS):
        rounded = amplitudes.astype(jnp.bfloat16)
        outgoing = rounded.at[wanted].get(mode="promise_in_bounds")
        arrived = lax.all_to_all(outgoing, PAIRS, 0, 0, tiled=True)
        last = iteration == ITERS - 1
        kept, *parts = couple(sched, weights, arrived, pieces, coup, not last)
        coupled = sum_parts(kept, parts)
        if not last:
            coupled = jnp.pad(coupled, ((0, 0), (0, 0), (0, lanes)))
            amplitudes = -(integral_f + coupled) / strip_denominator
    denominator = orbital_energy[:, :, None] + orbital_energy[:, None, :] + pair_energy[:, None, None]
    return -(integrals.astype(jnp.float32) + jnp.transpose(coupled)[None]) / denominator


def solution(mesh):
    split = Mesh(
        mesh.devices.reshape(4, 4, 2, mesh.shape["coup"]), ("pairs_0", "pairs_1", "pairs_2", "coup")
    )
    in_specs = (
        P(None, PAIRS),
        P(),
        P(PAIRS),
        P(PAIRS_COUP, None, None),
        P(PAIRS_COUP, None),
        P(PAIRS_COUP),
        P(PAIRS_COUP, None, None),
    )
    return jax.shard_map(
        amplitudes_of, mesh=split, in_specs=in_specs, out_specs=P(PAIRS_COUP, None, None), check_vma=False
    )
```

```python
import functools

import jax
import jax.numpy as jnp
from jax import lax
from jax.experimental import pallas as pl
from jax.experimental.pallas import tpu as pltpu
from jax.sharding import Mesh
from jax.sharding import PartitionSpec as P


ITERS = 2
PAIRS = ("pairs_0", "pairs_1", "pairs_2")
PAIRS_COUP = ("pairs_0", "pairs_1", "pairs_2", "coup")


def lookup(lookup_table, queries):
    columns = lax.broadcasted_iota(jnp.int32, (queries.shape[0], lookup_table.shape[0]), 1)
    return jnp.sum(jnp.where(queries[:, None] == columns, lookup_table[None, :], 0), axis=1)


def shift(x, step):
    peers = lax.axis_size("coup")
    return lax.ppermute(x, "coup", [(i, (i + step) % peers) for i in range(peers)])


def exchange_wanted(wanted_here):
    tiles = wanted_here.reshape(16, 2, 1)
    tiles = lax.all_to_all(tiles, "pairs_2", 1, 1, tiled=True)
    tiles = lax.all_to_all(tiles, ("pairs_0", "pairs_1"), 0, 0, tiled=True)
    return tiles.reshape(32)


def couple_kernel(first, slices, sched, weights, t_hbm, *refs):
    base, pieces = (0, refs[:7]) if first else (2 * t_hbm.shape[0], refs[:7])
    refs = refs[7:]
    if not first:
        running, refs = refs[0], refs[1:]
    outs, refs = (refs[:1], refs[1:]) if first else (refs[:4], refs[4:])
    acc, t_buf, o_buf, even_0, even_1, odd_0, odd_1, sems = refs
    sources, strip = t_buf.shape[0], t_buf.shape[1]
    count = 4 * sources
    offset = pl.multiple_of(sched[2 * count], 16)
    lane = pl.multiple_of(sched[2 * count + 1], 128)
    member = sched[2 * count + 2]
    copies, row = [], 0
    for i, piece in enumerate(pieces):
        size = piece.shape[0]
        copies.append(pltpu.make_async_copy(piece, o_buf.at[pl.ds(row, size)], sems.at[i]))
        row += size
    copies.append(pltpu.make_async_copy(t_hbm, t_buf, sems.at[7]))
    if not first:
        copies.append(pltpu.make_async_copy(running, acc, sems.at[8]))
    for copy in copies:
        copy.start()
    for ref in (even_0, even_1, odd_0, odd_1):
        ref[...] = jnp.zeros_like(ref)
    if first:
        acc[...] = jnp.zeros_like(acc)
    for copy in copies:
        copy.wait()

    def right(h, s, ref):
        product = lax.dot_general(
            t_buf[h], o_buf[sched[base + 2 * h + s]], (((1,), (1,)), ((), ())),
            preferred_element_type=jnp.float32,
        )
        ref[pl.ds(offset, strip), :] = product.astype(jnp.bfloat16)

    def left(h, s, ref):
        k = base + 2 * h + s
        product = jnp.dot(
            o_buf[sched[k], :, pl.ds(lane, 256)], ref[...], preferred_element_type=jnp.float32
        )
        acc[sched[count + k]] += weights[k] * product

    right(0, 0, even_0)
    right(0, 1, even_1)

    def step(i, carry):
        h = 2 * i
        right(h + 1, 0, odd_0)
        left(h, 0, even_0)
        right(h + 1, 1, odd_1)
        left(h, 1, even_1)
        after = jnp.minimum(h + 2, sources - 1)
        right(after, 0, even_0)
        left(h + 1, 0, odd_0)
        right(after, 1, even_1)
        left(h + 1, 1, odd_1)
        return carry

    lax.fori_loop(0, sources // 2, step, 0)
    if first:
        copy = pltpu.make_async_copy(acc, outs[0], sems.at[8])
        copy.start()
        copy.wait()
        return
    members = acc.shape[0]
    for d, out in enumerate(outs):
        peer = lax.rem(member + d, members)
        if slices:
            rows = pl.ds(pl.multiple_of(peer * strip, 16), strip)
            for r in range(members):
                out[r] = acc[lax.rem(peer + r, members), rows, :].astype(out.dtype)
        else:
            out[...] = acc[peer].astype(out.dtype)


def couple(sched, weights, strips, pieces, coup, running, slices):
    _, strip, lanes = strips.shape
    width = pieces[0].shape[1]
    first = running is None
    part = (coup, strip, width) if slices else (width, width)
    total = sum(piece.shape[0] for piece in pieces)
    anywhere = pl.BlockSpec(memory_space=pl.ANY)
    whole = pl.BlockSpec(part, lambda i, *_: (0,) * len(part))
    half = pltpu.VMEM((256, width), jnp.bfloat16)
    sums = jax.ShapeDtypeStruct((coup, width, width), jnp.float32)
    parts = [jax.ShapeDtypeStruct(part, jnp.float32)] + [jax.ShapeDtypeStruct(part, jnp.bfloat16)] * 3
    return pl.pallas_call(
        functools.partial(couple_kernel, first, slices),
        out_shape=[sums] if first else parts,
        grid_spec=pltpu.PrefetchScalarGridSpec(
            num_scalar_prefetch=2,
            grid=(1,),
            in_specs=[anywhere] * (1 + len(pieces) + (0 if first else 1)),
            out_specs=[anywhere] if first else [whole] * 4,
            scratch_shapes=[
                pltpu.VMEM((coup, width, width), jnp.float32),
                pltpu.VMEM(strips.shape, jnp.bfloat16),
                pltpu.VMEM((total, width, lanes), jnp.bfloat16),
                half, half, half, half,
                pltpu.SemaphoreType.DMA((9,)),
            ],
        ),
        compiler_params=pltpu.CompilerParams(vmem_limit_bytes=60 * 2**20),
        name="couple_first" if first else "couple_strips" if slices else "couple_pairs",
    )(sched, weights, strips, *pieces, *([] if first else [running]))


def sum_parts(kept, parts):
    for d, part in enumerate(parts):
        kept = kept + shift(part, d + 1).astype(jnp.float32)
    return kept


def amplitudes_of(
    coupling_list, pair_slot, coupling_weight, integrals, orbital_energy, pair_energy, intersections
):
    groups = lax.axis_size(PAIRS)
    coup = lax.axis_size("coup")
    group_index = lax.axis_index(PAIRS)
    member = lax.axis_index("coup")
    ov_dev, width = intersections.shape[0], integrals.shape[-1]
    count = coupling_list.shape[1]
    strip = width // coup
    lanes = -width % 128

    half = ov_dev // 2
    padded = jnp.pad(intersections, ((0, 0), (0, 0), (0, lanes)))
    low, high = padded[:half], padded[half:]
    last_low, next_high = shift(low, 1), shift(high, -1)
    last_high, next_low = shift(high, 1), shift(low, -1)
    far_low, far_high = shift(last_low, 1), shift(next_high, -1)
    pieces = (padded, next_low, next_high, far_low, far_high, last_low, last_high)

    owner_row = lookup(pair_slot, coupling_list[0]) - group_index * coup
    reader_row = lookup(pair_slot, coupling_list[1])
    source, read_pair = reader_row // coup, reader_row % coup
    local_o = coupling_list[2] - group_index * (ov_dev * coup)
    local_o = (local_o - member * ov_dev) % (ov_dev * coup)
    position = lax.iota(jnp.int32, count)
    twin = jnp.max(
        jnp.where((source[None, :] == source[:, None]) & (position[None, :] < position[:, None]), 1, 0), axis=1
    )
    core = lax.axis_index("pairs_2")
    slot = groups * (source % 2 ^ core) + source // 2 * 2 + twin
    chosen = slot[None, :] == position[:, None]
    pick = lambda v: jnp.sum(jnp.where(chosen, v[None, :], jnp.zeros((), v.dtype)), axis=1)
    strip_row = member * strip
    lane_tile = jnp.minimum(strip_row // 128, 2) * 128
    sched = jnp.concatenate(
        [pick(local_o), pick(owner_row), jnp.stack([strip_row - lane_tile, lane_tile, member])]
    ).astype(jnp.int32)
    weights = pick(coupling_weight)
    asked = source[None, :] == lax.broadcasted_iota(jnp.int32, (groups, count), 0)
    wanted = exchange_wanted(jnp.max(jnp.where(asked, read_pair[None, :], 0), axis=1))

    denominator = orbital_energy[:, :, None] + orbital_energy[:, None, :] + pair_energy[:, None, None]
    own_integrals = integrals.astype(jnp.float32)

    def to_strips(matrix):
        flipped = jnp.pad(jnp.transpose(matrix), ((0, 0), (0, lanes)))
        rows_of = lambda d: lax.dynamic_slice_in_dim(flipped, lax.rem(member + d, coup) * strip, strip)
        return jnp.stack([rows_of(0)] + [shift(rows_of(coup - e), coup - e) for e in range(1, coup)])

    rounded = to_strips((-own_integrals / denominator).astype(jnp.bfloat16)[0])
    integral_strips = to_strips(integrals[0])
    energies = jnp.concatenate([orbital_energy[0], pair_energy])[None]
    energies = jnp.concatenate([energies] + [shift(energies, -e) for e in range(1, coup)])
    orbital, pair = energies[:, :width], energies[:, width]
    own_rows = lax.dynamic_slice_in_dim(orbital, strip_row, strip, axis=1)
    all_columns = jnp.pad(orbital, ((0, 0), (0, lanes)))
    strip_denominator = own_rows[:, :, None] + all_columns[:, None, :] + pair[:, None, None]
    wanted = ((wanted - member) % coup).reshape(groups // 2, 2)
    wanted_same = jnp.where(core == 0, wanted[:, 0], wanted[:, 1])
    wanted_other = jnp.where(core == 0, wanted[:, 1], wanted[:, 0])

    for iteration in range(ITERS):
        last = iteration == ITERS - 1
        other = rounded.at[wanted_other].get(mode="promise_in_bounds")
        other = lax.ppermute(other, "pairs_2", [(0, 1), (1, 0)])
        same = rounded.at[wanted_same].get(mode="promise_in_bounds")
        same = lax.all_to_all(same, PAIRS[:2], 0, 0, tiled=True)
        other = lax.all_to_all(other, PAIRS[:2], 0, 0, tiled=True)
        (running,) = couple(sched, weights, same, pieces, coup, None, not last)
        kept, *parts = couple(sched, weights, other, pieces, coup, running, not last)
        coupled = sum_parts(kept, parts)
        if not last:
            coupled = jnp.pad(coupled, ((0, 0), (0, 0), (0, lanes)))
            amplitudes = -(integral_strips.astype(jnp.float32) + coupled) / strip_denominator
            rounded = amplitudes.astype(jnp.bfloat16)
    return -(own_integrals + jnp.transpose(coupled)[None]) / denominator


def solution(mesh):
    split = Mesh(
        mesh.devices.reshape(4, 4, 2, mesh.shape["coup"]), ("pairs_0", "pairs_1", "pairs_2", "coup")
    )
    in_specs = (
        P(None, PAIRS),
        P(),
        P(PAIRS),
        P(PAIRS_COUP, None, None),
        P(PAIRS_COUP, None),
        P(PAIRS_COUP),
        P(PAIRS_COUP, None, None),
    )
    return jax.shard_map(
        amplitudes_of, mesh=split, in_specs=in_specs, out_specs=P(PAIRS_COUP, None, None), check_vma=False
    )
```

```python
import functools

import jax
import jax.numpy as jnp
from jax import lax
from jax.experimental import pallas as pl
from jax.experimental.pallas import tpu as pltpu
from jax.sharding import Mesh
from jax.sharding import PartitionSpec as P


ITERS = 2
PAIRS = ("pairs_0", "pairs_1", "pairs_2")
PAIRS_COUP = ("pairs_0", "pairs_1", "pairs_2", "coup")


def lookup(lookup_table, queries):
    columns = lax.broadcasted_iota(jnp.int32, (queries.shape[0], lookup_table.shape[0]), 1)
    return jnp.sum(jnp.where(queries[:, None] == columns, lookup_table[None, :], 0), axis=1)


def shift(x, step):
    peers = lax.axis_size("coup")
    return lax.ppermute(x, "coup", [(i, (i + step) % peers) for i in range(peers)])


def exchange_wanted(wanted_here):
    return lax.all_to_all(wanted_here[:, None, None], PAIRS, 0, 0, tiled=True)[:, 0, 0]


def pack(x, lead):
    whole = x.shape[-1] // 128 * 128
    tiles = [x[..., t : t + 128] for t in range(0, whole, 128)]
    tail = x[..., whole:]
    tiles.append(jnp.concatenate([tail[..., :lead, :], tail[..., -lead:, :]], axis=-1))
    return jnp.concatenate(tiles, axis=-2)


def couple_kernel(
    slices, sched, weights, t_hbm, o_own, o_1, o_2, o_3, o_4, o_5, o_6, kept, out_1, out_2, out_3,
    acc, t_buf, o_buf, t_tail, o_tail, even_0, even_1, odd_0, odd_1, sems,
):
    sources, strip, width = t_buf.shape[0], t_buf.shape[1], o_buf.shape[1]
    full = width // 128
    o_lead, t_lead = o_tail.shape[1], t_tail.shape[1]
    count = 2 * sources
    offset = pl.multiple_of(sched[2 * count], 16)
    lane = pl.multiple_of(sched[2 * count + 1], 128)
    member = sched[2 * count + 2]
    copies, first = [], 0
    for piece in (o_own, o_1, o_2, o_3, o_4, o_5, o_6):
        size = piece.shape[0]
        into = pl.ds(first, size)
        for t in range(full):
            copies.append((piece.at[:, pl.ds(t * width, width), :], o_buf.at[into, :, pl.ds(128 * t, 128)]))
        copies.append((piece.at[:, pl.ds(full * width, o_lead), :], o_tail.at[into]))
        first += size
    for t in range(full):
        copies.append((t_hbm.at[:, pl.ds(t * strip, strip), :], t_buf.at[:, :, pl.ds(128 * t, 128)]))
    copies.append((t_hbm.at[:, pl.ds(full * strip, t_lead), :], t_tail))
    copies = [pltpu.make_async_copy(src, dst, sems.at[i]) for i, (src, dst) in enumerate(copies)]
    for copy in copies:
        copy.start()
    for ref in (acc, even_0, even_1, odd_0, odd_1):
        ref[...] = jnp.zeros_like(ref)
    for copy in copies:
        copy.wait()

    def unpack(tail, buf, index, lead):
        both = tail[index]
        empty = jnp.zeros((lead, 64), both.dtype)
        rows = buf.shape[1]
        buf[index, 0:lead, 128 * full :] = jnp.concatenate([both[:, :64], empty], axis=1)
        buf[index, rows - lead : rows, 128 * full :] = jnp.concatenate([both[:, 64:], empty], axis=1)

    def unpack_o(i, carry):
        unpack(o_tail, o_buf, i, o_lead)
        unpack(t_tail, t_buf, 2 * i, t_lead)
        unpack(t_tail, t_buf, 2 * i + 1, t_lead)
        return carry

    lax.fori_loop(0, sources // 2, unpack_o, 0)

    def right(h, s, ref):
        product = lax.dot_general(
            t_buf[h], o_buf[sched[2 * h + s]], (((1,), (1,)), ((), ())), preferred_element_type=jnp.float32
        )
        ref[pl.ds(offset, strip), :] = product.astype(jnp.bfloat16)

    def left(h, s, ref):
        k = 2 * h + s
        product = jnp.dot(
            o_buf[sched[k], :, pl.ds(lane, 256)], ref[...], preferred_element_type=jnp.float32
        )
        acc[sched[count + k]] += weights[k] * product

    right(0, 0, even_0)
    right(0, 1, even_1)

    def step(i, carry):
        h = 2 * i
        right(h + 1, 0, odd_0)
        left(h, 0, even_0)
        right(h + 1, 1, odd_1)
        left(h, 1, even_1)
        after = jnp.minimum(h + 2, sources - 1)
        right(after, 0, even_0)
        left(h + 1, 0, odd_0)
        right(after, 1, even_1)
        left(h + 1, 1, odd_1)
        return carry

    lax.fori_loop(0, sources // 2, step, 0)
    members = acc.shape[0]
    for d, out in enumerate((kept, out_1, out_2, out_3)):
        peer = lax.rem(member + d, members)
        if slices:
            begin = pl.multiple_of(peer * strip, 16)
            for r in range(members):
                row = lax.rem(peer + r, members)
                for t in range(full):
                    part = acc[row, pl.ds(begin, strip), 128 * t : 128 * t + 128]
                    out[r, strip * t : strip * t + strip, :] = part.astype(out.dtype)
                tail = acc[row, pl.ds(begin, strip), 128 * full :]
                out[r, strip * full :, :] = jnp.concatenate(
                    [tail[:t_lead], tail[strip - t_lead :]], axis=1
                ).astype(out.dtype)
        else:
            out[...] = acc[peer].astype(out.dtype)


def couple(sched, weights, strips, pieces, coup, strip, width, slices):
    sources, packed, _ = strips.shape
    full = width // 128
    lanes = 128 * full + 128
    part = (coup, packed, 128) if slices else (width, width)
    total = sum(piece.shape[0] for piece in pieces)
    whole = pl.BlockSpec(part, lambda i, *_: (0,) * len(part))
    half = pltpu.VMEM((256, width), jnp.bfloat16)
    return pl.pallas_call(
        functools.partial(couple_kernel, slices),
        out_shape=[jax.ShapeDtypeStruct(part, jnp.float32)] + [jax.ShapeDtypeStruct(part, jnp.bfloat16)] * 3,
        grid_spec=pltpu.PrefetchScalarGridSpec(
            num_scalar_prefetch=2,
            grid=(1,),
            in_specs=[pl.BlockSpec(memory_space=pl.ANY)] * (1 + len(pieces)),
            out_specs=[whole] * 4,
            scratch_shapes=[
                pltpu.VMEM((coup, width, width), jnp.float32),
                pltpu.VMEM((sources, strip, lanes), jnp.bfloat16),
                pltpu.VMEM((total, width, lanes), jnp.bfloat16),
                pltpu.VMEM((sources, packed - full * strip, 128), jnp.bfloat16),
                pltpu.VMEM((total, width // 2, 128), jnp.bfloat16),
                half, half, half, half,
                pltpu.SemaphoreType.DMA(((full + 1) * (len(pieces) + 1),)),
            ],
        ),
        compiler_params=pltpu.CompilerParams(vmem_limit_bytes=60 * 2**20),
        name="couple_strips" if slices else "couple_pairs",
    )(sched, weights, strips, *pieces)


def sum_parts(kept, parts):
    for d, part in enumerate(parts):
        kept = kept + shift(part, d + 1).astype(jnp.float32)
    return kept


def amplitudes_of(
    coupling_list, pair_slot, coupling_weight, integrals, orbital_energy, pair_energy, intersections
):
    groups = lax.axis_size(PAIRS)
    coup = lax.axis_size("coup")
    group_index = lax.axis_index(PAIRS)
    member = lax.axis_index("coup")
    ov_dev, width = intersections.shape[0], integrals.shape[-1]
    count = coupling_list.shape[1]
    strip = width // coup
    lead = -(-strip // 2 // 16) * 16

    half = ov_dev // 2
    packed = pack(intersections, width // 2)
    low, high = packed[:half], packed[half:]
    last_low, next_high = shift(low, 1), shift(high, -1)
    last_high, next_low = shift(high, 1), shift(low, -1)
    far_low, far_high = shift(last_low, 1), shift(next_high, -1)
    pieces = (packed, next_low, next_high, far_low, far_high, last_low, last_high)

    owner_row = lookup(pair_slot, coupling_list[0]) - group_index * coup
    reader_row = lookup(pair_slot, coupling_list[1])
    source, read_pair = reader_row // coup, reader_row % coup
    local_o = coupling_list[2] - group_index * (ov_dev * coup)
    local_o = (local_o - member * ov_dev) % (ov_dev * coup)
    position = lax.iota(jnp.int32, count)
    twin = jnp.max(
        jnp.where((source[None, :] == source[:, None]) & (position[None, :] < position[:, None]), 1, 0), axis=1
    )
    slot = 2 * source + twin
    chosen = slot[None, :] == position[:, None]
    pick = lambda v: jnp.sum(jnp.where(chosen, v[None, :], jnp.zeros((), v.dtype)), axis=1)
    strip_row = member * strip
    lane_tile = jnp.minimum(strip_row // 128, 2) * 128
    sched = jnp.concatenate(
        [pick(local_o), pick(owner_row), jnp.stack([strip_row - lane_tile, lane_tile, member])]
    ).astype(jnp.int32)
    weights = pick(coupling_weight)
    asked = source[None, :] == lax.broadcasted_iota(jnp.int32, (groups, count), 0)
    wanted = exchange_wanted(jnp.max(jnp.where(asked, read_pair[None, :], 0), axis=1))

    denominator = orbital_energy[:, :, None] + orbital_energy[:, None, :] + pair_energy[:, None, None]
    own_integrals = integrals.astype(jnp.float32)

    def to_strips(matrix):
        tiles = pack(jnp.transpose(matrix).reshape(coup, strip, width), lead)
        part = lambda d: lax.dynamic_index_in_dim(tiles, lax.rem(member + d, coup), keepdims=False)
        return jnp.stack([part(0)] + [shift(part(coup - e), coup - e) for e in range(1, coup)])

    rounded = to_strips((-own_integrals / denominator).astype(jnp.bfloat16)[0])
    integral_strips = to_strips(integrals[0])
    energies = jnp.concatenate([orbital_energy[0], pair_energy])[None]
    energies = jnp.concatenate([energies] + [shift(energies, -e) for e in range(1, coup)])
    orbital, pair = energies[:, :width], energies[:, width]
    own_rows = lax.dynamic_slice_in_dim(orbital, strip_row, strip, axis=1)
    strip_denominator = pack(own_rows[:, :, None] + orbital[:, None, :] + pair[:, None, None], lead)
    wanted = (wanted - member) % coup

    for iteration in range(ITERS):
        outgoing = rounded.at[wanted].get(mode="promise_in_bounds")
        arrived = lax.all_to_all(outgoing, PAIRS, 0, 0, tiled=True)
        last = iteration == ITERS - 1
        kept, *parts = couple(sched, weights, arrived, pieces, coup, strip, width, not last)
        coupled = sum_parts(kept, parts)
        if not last:
            amplitudes = -(integral_strips.astype(jnp.float32) + coupled) / strip_denominator
            rounded = amplitudes.astype(jnp.bfloat16)
    return -(own_integrals + jnp.transpose(coupled)[None]) / denominator


def solution(mesh):
    split = Mesh(
        mesh.devices.reshape(4, 4, 2, mesh.shape["coup"]), ("pairs_0", "pairs_1", "pairs_2", "coup")
    )
    in_specs = (
        P(None, PAIRS),
        P(),
        P(PAIRS),
        P(PAIRS_COUP, None, None),
        P(PAIRS_COUP, None),
        P(PAIRS_COUP),
        P(PAIRS_COUP, None, None),
    )
    return jax.shard_map(
        amplitudes_of, mesh=split, in_specs=in_specs, out_specs=P(PAIRS_COUP, None, None), check_vma=False
    )
```

```python
import functools

import jax
import jax.numpy as jnp
from jax import lax
from jax.experimental import pallas as pl
from jax.experimental.pallas import tpu as pltpu
from jax.sharding import Mesh
from jax.sharding import PartitionSpec as P


ITERS = 2
PAIRS = ("pairs_0", "pairs_1", "pairs_2")
PAIRS_COUP = ("pairs_0", "pairs_1", "pairs_2", "coup")


def lookup(lookup_table, queries):
    columns = lax.broadcasted_iota(jnp.int32, (queries.shape[0], lookup_table.shape[0]), 1)
    return jnp.sum(jnp.where(queries[:, None] == columns, lookup_table[None, :], 0), axis=1)


def shift(x, step):
    peers = lax.axis_size("coup")
    return lax.ppermute(x, "coup", [(i, (i + step) % peers) for i in range(peers)])


def exchange_wanted(wanted_here):
    return lax.all_to_all(wanted_here[:, None, None], PAIRS, 0, 0, tiled=True)[:, 0, 0]


def pack(x, lead):
    whole = x.shape[-1] // 128 * 128
    tiles = [x[..., t : t + 128] for t in range(0, whole, 128)]
    tail = x[..., whole:]
    tiles.append(jnp.concatenate([tail[..., :lead, :], tail[..., -lead:, :]], axis=-1))
    return jnp.concatenate(tiles, axis=-2)


def couple_kernel(distances, slices, unroll, sched, weights, t_hbm, o_own, o_1, o_2, o_3, o_4, o_5, o_6, *refs):
    outs, refs = refs[: len(distances)], refs[len(distances) :]
    acc, t_buf, o_buf, t_tail, o_tail, even_0, even_1, odd_0, odd_1, sems = refs
    sources, strip, width = t_buf.shape[0], t_buf.shape[1], o_buf.shape[1]
    full = width // 128
    o_lead, t_lead = o_tail.shape[1], t_tail.shape[1]
    count = 2 * sources
    offset = pl.multiple_of(sched[3 * count], 16)
    lane = pl.multiple_of(sched[3 * count + 1], 128)
    member = sched[3 * count + 2]
    begin, turns = sched[3 * count + 3], sched[3 * count + 4]
    copies, first = [], 0
    for piece in (o_own, o_1, o_2, o_3, o_4, o_5, o_6):
        size = piece.shape[0]
        into = pl.ds(first, size)
        for t in range(full):
            copies.append((piece.at[:, pl.ds(t * width, width), :], o_buf.at[into, :, pl.ds(128 * t, 128)]))
        copies.append((piece.at[:, pl.ds(full * width, o_lead), :], o_tail.at[into]))
        first += size
    for t in range(full):
        copies.append((t_hbm.at[:, pl.ds(t * strip, strip), :], t_buf.at[:, :, pl.ds(128 * t, 128)]))
    copies.append((t_hbm.at[:, pl.ds(full * strip, t_lead), :], t_tail))
    copies = [pltpu.make_async_copy(src, dst, sems.at[i]) for i, (src, dst) in enumerate(copies)]
    for copy in copies:
        copy.start()
    for ref in (acc, even_0, even_1, odd_0, odd_1):
        ref[...] = jnp.zeros_like(ref)
    for copy in copies:
        copy.wait()

    def unpack(tail, buf, index, lead):
        both = tail[index]
        empty = jnp.zeros((lead, 64), both.dtype)
        rows = buf.shape[1]
        buf[index, 0:lead, 128 * full :] = jnp.concatenate([both[:, :64], empty], axis=1)
        buf[index, rows - lead : rows, 128 * full :] = jnp.concatenate([both[:, 64:], empty], axis=1)

    def unpack_o(i, carry):
        unpack(o_tail, o_buf, i, o_lead)
        unpack(t_tail, t_buf, 2 * i, t_lead)
        unpack(t_tail, t_buf, 2 * i + 1, t_lead)
        return carry

    lax.fori_loop(0, sources // 2, unpack_o, 0)

    def right(k, ref):
        k = jnp.minimum(k, count - 1)
        product = lax.dot_general(
            t_buf[sched[2 * count + k]], o_buf[sched[k]], (((1,), (1,)), ((), ())),
            preferred_element_type=jnp.float32,
        )
        ref[pl.ds(offset, strip), :] = product.astype(jnp.bfloat16)

    def left(k, ref):
        product = jnp.dot(
            o_buf[sched[k], :, pl.ds(lane, 256)], ref[...], preferred_element_type=jnp.float32
        )
        acc[sched[count + k]] += weights[k] * product

    right(begin, even_0)
    right(begin + 1, even_1)

    def turn(i, carry):
        for u in range(unroll):
            k = begin + 4 * (unroll * i + u)
            right(k + 2, odd_0)
            left(k, even_0)
            right(k + 3, odd_1)
            left(k + 1, even_1)
            right(k + 4, even_0)
            left(k + 2, odd_0)
            right(k + 5, even_1)
            left(k + 3, odd_1)
        return carry

    lax.fori_loop(0, turns, turn, 0)
    members = acc.shape[0]
    for d, out in zip(distances, outs):
        peer = lax.rem(member + d, members)
        if slices:
            rows = pl.ds(pl.multiple_of(peer * strip, 16), strip)
            for r in range(members):
                row = lax.rem(peer + r, members)
                for t in range(full):
                    part = acc[row, rows, 128 * t : 128 * t + 128]
                    out[r, strip * t : strip * t + strip, :] = part.astype(out.dtype)
                tail = acc[row, rows, 128 * full :]
                out[r, strip * full :, :] = jnp.concatenate(
                    [tail[:t_lead], tail[strip - t_lead :]], axis=1
                ).astype(out.dtype)
        else:
            out[...] = acc[peer].astype(out.dtype)


def couple(sched, weights, strips, pieces, coup, strip, width, distances, slices, unroll):
    sources, packed, _ = strips.shape
    full = width // 128
    lanes = 128 * full + 128
    part = (coup, packed, 128) if slices else (width, width)
    total = sum(piece.shape[0] for piece in pieces)
    whole = pl.BlockSpec(part, lambda i, *_: (0,) * len(part))
    half = pltpu.VMEM((256, width), jnp.bfloat16)
    return pl.pallas_call(
        functools.partial(couple_kernel, distances, slices, unroll),
        out_shape=[jax.ShapeDtypeStruct(part, jnp.bfloat16 if d else jnp.float32) for d in distances],
        grid_spec=pltpu.PrefetchScalarGridSpec(
            num_scalar_prefetch=2,
            grid=(1,),
            in_specs=[pl.BlockSpec(memory_space=pl.ANY)] * (1 + len(pieces)),
            out_specs=[whole] * len(distances),
            scratch_shapes=[
                pltpu.VMEM((coup, width, width), jnp.float32),
                pltpu.VMEM((sources, strip, lanes), jnp.bfloat16),
                pltpu.VMEM((total, width, lanes), jnp.bfloat16),
                pltpu.VMEM((sources, packed - full * strip, 128), jnp.bfloat16),
                pltpu.VMEM((total, width // 2, 128), jnp.bfloat16),
                half, half, half, half,
                pltpu.SemaphoreType.DMA(((full + 1) * (len(pieces) + 1),)),
            ],
        ),
        compiler_params=pltpu.CompilerParams(vmem_limit_bytes=60 * 2**20),
    )(sched, weights, strips, *pieces)


def amplitudes_of(
    coupling_list, pair_slot, coupling_weight, integrals, orbital_energy, pair_energy, intersections
):
    groups = lax.axis_size(PAIRS)
    coup = lax.axis_size("coup")
    group_index = lax.axis_index(PAIRS)
    member = lax.axis_index("coup")
    ov_dev, width = intersections.shape[0], integrals.shape[-1]
    count = coupling_list.shape[1]
    strip = width // coup
    lead = -(-strip // 2 // 16) * 16

    half = ov_dev // 2
    packed = pack(intersections, width // 2)
    low, high = packed[:half], packed[half:]
    last_low, next_high = shift(low, 1), shift(high, -1)
    last_high, next_low = shift(high, 1), shift(low, -1)
    far_low, far_high = shift(last_low, 1), shift(next_high, -1)
    pieces = (packed, next_low, next_high, far_low, far_high, last_low, last_high)

    owner_row = lookup(pair_slot, coupling_list[0]) - group_index * coup
    reader_row = lookup(pair_slot, coupling_list[1])
    source, read_pair = reader_row // coup, reader_row % coup
    local_o = coupling_list[2] - group_index * (ov_dev * coup)
    local_o = (local_o - member * ov_dev) % (ov_dev * coup)
    position = lax.iota(jnp.int32, count)
    twin = jnp.max(
        jnp.where((source[None, :] == source[:, None]) & (position[None, :] < position[:, None]), 1, 0), axis=1
    )
    slot = 2 * source + twin
    chosen = slot[None, :] == position[:, None]
    pick = lambda chosen, v: jnp.sum(jnp.where(chosen, v[None, :], jnp.zeros((), v.dtype)), axis=1)
    strip_row = member * strip
    lane_tile = jnp.minimum(strip_row // 128, 2) * 128
    place = [strip_row - lane_tile, lane_tile, member]

    def schedule(chosen, *bounds):
        columns = [pick(chosen, v) for v in (local_o, owner_row, source)]
        return jnp.concatenate([*columns, jnp.stack([*place, *bounds])]).astype(jnp.int32)

    by_source = schedule(chosen, jnp.int32(0), jnp.int32(count // 16))
    weights = pick(chosen, coupling_weight)
    distance = (owner_row - member) % coup
    outer = (distance == 1) | (distance == 2)
    before = position[None, :] < position[:, None]
    ahead = jnp.sum(jnp.where(outer[None, :] & (before | ~outer[:, None]), 1, 0), axis=1)
    behind = jnp.sum(jnp.where(~outer[None, :] & before, 1, 0), axis=1)
    chosen = jnp.where(outer, ahead, ahead + behind)[None, :] == position[:, None]
    outer_count = jnp.sum(jnp.where(outer, 1, 0))
    outer_turns, inner_begin = (outer_count + 3) // 4, outer_count // 4 * 4
    by_row_outer = schedule(chosen, jnp.int32(0), outer_turns)
    by_row_inner = schedule(chosen, inner_begin, (count - inner_begin) // 4)
    weights_outer = pick(chosen, jnp.where(outer, coupling_weight, 0.0))
    weights_inner = pick(chosen, jnp.where(outer, 0.0, coupling_weight))
    asked = source[None, :] == lax.broadcasted_iota(jnp.int32, (groups, count), 0)
    wanted = exchange_wanted(jnp.max(jnp.where(asked, read_pair[None, :], 0), axis=1))

    denominator = orbital_energy[:, :, None] + orbital_energy[:, None, :] + pair_energy[:, None, None]
    own_integrals = integrals.astype(jnp.float32)

    def to_strips(matrix):
        tiles = pack(jnp.transpose(matrix).reshape(coup, strip, width), lead)
        part = lambda d: lax.dynamic_index_in_dim(tiles, lax.rem(member + d, coup), keepdims=False)
        return jnp.stack([part(0)] + [shift(part(coup - e), coup - e) for e in range(1, coup)])

    rounded = to_strips((-own_integrals / denominator).astype(jnp.bfloat16)[0])
    integral_strips = to_strips(integrals[0])
    energies = jnp.concatenate([orbital_energy[0], pair_energy])[None]
    energies = jnp.concatenate([energies] + [shift(energies, -e) for e in range(1, coup)])
    orbital, pair = energies[:, :width], energies[:, width]
    own_rows = lax.dynamic_slice_in_dim(orbital, strip_row, strip, axis=1)
    strip_denominator = pack(own_rows[:, :, None] + orbital[:, None, :] + pair[:, None, None], lead)
    wanted = (wanted - member) % coup

    def exchange(rounded):
        outgoing = rounded.at[wanted].get(mode="promise_in_bounds")
        arrived = lax.all_to_all(outgoing, PAIRS, 0, 0, tiled=True)
        return pltpu.with_memory_space_constraint(arrived, pltpu.HBM)

    for _ in range(ITERS - 1):
        arrived = exchange(rounded)
        kept, *parts = couple(by_source, weights, arrived, pieces, coup, strip, width, (0, 1, 2, 3), True, 4)
        for d, part in enumerate(parts):
            kept = kept + shift(part, d + 1).astype(jnp.float32)
        amplitudes = -(integral_strips.astype(jnp.float32) + kept) / strip_denominator
        rounded = amplitudes.astype(jnp.bfloat16)

    arrived = exchange(rounded)
    part_2, part_1 = couple(
        by_row_outer, weights_outer, arrived, pieces, coup, strip, width, (2, 1), False, 1
    )
    part_2, part_1 = shift(part_2, 2), shift(part_1, 1)
    part_3, kept = couple(
        by_row_inner, weights_inner, arrived, pieces, coup, strip, width, (3, 0), False, 1
    )
    part_3 = shift(part_3, 3)
    coupled = kept
    for part in (part_1, part_2, part_3):
        coupled = coupled + part.astype(jnp.float32)
    return -(own_integrals + jnp.transpose(coupled)[None]) / denominator


def solution(mesh):
    split = Mesh(
        mesh.devices.reshape(4, 4, 2, mesh.shape["coup"]), ("pairs_0", "pairs_1", "pairs_2", "coup")
    )
    in_specs = (
        P(None, PAIRS),
        P(),
        P(PAIRS),
        P(PAIRS_COUP, None, None),
        P(PAIRS_COUP, None),
        P(PAIRS_COUP),
        P(PAIRS_COUP, None, None),
    )
    return jax.shard_map(
        amplitudes_of, mesh=split, in_specs=in_specs, out_specs=P(PAIRS_COUP, None, None), check_vma=False
    )
```

```python
import functools

import jax
import jax.numpy as jnp
from jax import lax
from jax.experimental import pallas as pl
from jax.experimental.pallas import tpu as pltpu
from jax.sharding import Mesh
from jax.sharding import PartitionSpec as P


ITERS = 2
PAIRS = ("pairs_0", "pairs_1", "pairs_2")
PAIRS_COUP = ("pairs_0", "pairs_1", "pairs_2", "coup")


def lookup(lookup_table, queries):
    columns = lax.broadcasted_iota(jnp.int32, (queries.shape[0], lookup_table.shape[0]), 1)
    return jnp.sum(jnp.where(queries[:, None] == columns, lookup_table[None, :], 0), axis=1)


def shift(x, step):
    peers = lax.axis_size("coup")
    return lax.ppermute(x, "coup", [(i, (i + step) % peers) for i in range(peers)])


def exchange_wanted(wanted_here):
    return lax.all_to_all(wanted_here[:, None, None], PAIRS, 0, 0, tiled=True)[:, 0, 0]


def pack(x, lead):
    whole = x.shape[-1] // 128 * 128
    tiles = [x[..., t : t + 128] for t in range(0, whole, 128)]
    tail = x[..., whole:]
    tiles.append(jnp.concatenate([tail[..., :lead, :], tail[..., -lead:, :]], axis=-1))
    return jnp.concatenate(tiles, axis=-2)


def couple_kernel(slices, unroll, sched, weights, t_ref, *refs):
    if slices:
        pieces, outs, o_buf, refs = refs[:7], refs[7:11], refs[11], refs[12:]
        acc, t_tail, even_0, even_1, odd_0, odd_1, o_tail, sems = refs
    else:
        o_buf, outs, refs = refs[0], refs[1:5], refs[5:]
        acc, t_tail, even_0, even_1, odd_0, odd_1 = refs
    sources, strip, width = t_tail.shape[0], t_tail.shape[1], o_buf.shape[1]
    full = width // 128
    t_lead = t_ref.shape[1] - full * strip
    count = 2 * sources
    offset = pl.multiple_of(sched[2 * count], 16)
    lane = pl.multiple_of(sched[2 * count + 1], 128)
    member = sched[2 * count + 2]
    copies, first = [], 0
    if slices:
        o_lead = o_tail.shape[1]
        for piece in pieces:
            size = piece.shape[0]
            into = pl.ds(first, size)
            for t in range(full):
                copies.append((piece.at[:, pl.ds(t * width, width), :], o_buf.at[into, :, pl.ds(128 * t, 128)]))
            copies.append((piece.at[:, pl.ds(full * width, o_lead), :], o_tail.at[into]))
            first += size
        copies = [pltpu.make_async_copy(src, dst, sems.at[i]) for i, (src, dst) in enumerate(copies)]
        for copy in copies:
            copy.start()
    for ref in (acc, even_0, even_1, odd_0, odd_1):
        ref[...] = jnp.zeros_like(ref)

    def halves(both):
        empty = jnp.zeros((both.shape[0], 64), both.dtype)
        return jnp.concatenate([both[:, :64], empty], axis=1), jnp.concatenate([both[:, 64:], empty], axis=1)

    def unpack_t(h, carry):
        low, high = halves(t_ref[h, full * strip :, :])
        t_tail[h, 0:t_lead, :] = low
        t_tail[h, strip - t_lead :, :] = high
        return carry

    lax.fori_loop(0, sources, unpack_t, 0)
    for copy in copies:
        copy.wait()
    if slices:

        def unpack_o(i, carry):
            low, high = halves(o_tail[i])
            o_buf[i, 0:o_lead, 128 * full :] = low
            o_buf[i, width - o_lead :, 128 * full :] = high
            return carry

        lax.fori_loop(0, first, unpack_o, 0)

    def right(h, s, ref):
        tiles = [t_ref[h, strip * t : strip * t + strip, :] for t in range(full)] + [t_tail[h]]
        product = lax.dot_general(
            jnp.concatenate(tiles, axis=1), o_buf[sched[2 * h + s]], (((1,), (1,)), ((), ())),
            preferred_element_type=jnp.float32,
        )
        ref[pl.ds(offset, strip), :] = product.astype(jnp.bfloat16)

    def left(h, s, ref):
        k = 2 * h + s
        product = jnp.dot(
            o_buf[sched[k], :, pl.ds(lane, 256)], ref[...], preferred_element_type=jnp.float32
        )
        acc[sched[count + k]] += weights[k] * product

    right(0, 0, even_0)
    right(0, 1, even_1)

    def turn(i, carry):
        for u in range(unroll):
            h = 2 * (unroll * i + u)
            right(h + 1, 0, odd_0)
            left(h, 0, even_0)
            right(h + 1, 1, odd_1)
            left(h, 1, even_1)
            after = jnp.minimum(h + 2, sources - 1)
            right(after, 0, even_0)
            left(h + 1, 0, odd_0)
            right(after, 1, even_1)
            left(h + 1, 1, odd_1)
        return carry

    lax.fori_loop(0, sources // (2 * unroll), turn, 0)
    members = acc.shape[0]
    for d, out in enumerate(outs):
        peer = lax.rem(member + d, members)
        if slices:
            begin = pl.multiple_of(peer * strip, 16)
            for r in range(members):
                row = lax.rem(peer + r, members)
                for t in range(full):
                    part = acc[row, pl.ds(begin, strip), 128 * t : 128 * t + 128]
                    out[r, strip * t : strip * t + strip, :] = part.astype(out.dtype)
                tail = acc[row, pl.ds(begin, strip), 128 * full :]
                out[r, strip * full :, :] = jnp.concatenate(
                    [tail[:t_lead], tail[strip - t_lead :]], axis=1
                ).astype(out.dtype)
        else:
            out[...] = acc[peer].astype(out.dtype)


def couple(sched, weights, strips, held, coup, strip, width, slices):
    sources, packed, _ = strips.shape
    full = width // 128
    total = sum(piece.shape[0] for piece in held)
    part = (coup, packed, 128) if slices else (width, width)
    table = (total, width, 128 * full + 128)
    resident = pl.BlockSpec(memory_space=pltpu.VMEM)
    whole = pl.BlockSpec(part, lambda i, *_: (0,) * len(part))
    half = pltpu.VMEM((256, width), jnp.bfloat16)
    scratch = [
        pltpu.VMEM((coup, width, width), jnp.float32),
        pltpu.VMEM((sources, strip, 128), jnp.bfloat16),
        half, half, half, half,
    ]
    shapes = [jax.ShapeDtypeStruct(part, jnp.float32)] + [jax.ShapeDtypeStruct(part, jnp.bfloat16)] * 3
    if slices:
        scratch += [
            pltpu.VMEM((total, width // 2, 128), jnp.bfloat16),
            pltpu.SemaphoreType.DMA(((full + 1) * len(held),)),
        ]
        shapes.append(pltpu.VMEM(table, jnp.bfloat16))
    return pl.pallas_call(
        functools.partial(couple_kernel, slices, 4),
        out_shape=shapes,
        grid_spec=pltpu.PrefetchScalarGridSpec(
            num_scalar_prefetch=2,
            grid=(1,),
            in_specs=[resident] + ([pl.BlockSpec(memory_space=pl.ANY)] * len(held) if slices else [resident]),
            out_specs=[whole] * 4 + ([resident] if slices else []),
            scratch_shapes=scratch,
        ),
        compiler_params=pltpu.CompilerParams(vmem_limit_bytes=32 * 2**20),
        name="couple_strips" if slices else "couple_pairs",
    )(sched, weights, strips, *held)


def sum_parts(kept, parts):
    for d, part in enumerate(parts):
        kept = kept + shift(part, d + 1).astype(jnp.float32)
    return kept


def amplitudes_of(
    coupling_list, pair_slot, coupling_weight, integrals, orbital_energy, pair_energy, intersections
):
    groups = lax.axis_size(PAIRS)
    coup = lax.axis_size("coup")
    group_index = lax.axis_index(PAIRS)
    member = lax.axis_index("coup")
    ov_dev, width = intersections.shape[0], integrals.shape[-1]
    count = coupling_list.shape[1]
    strip = width // coup
    lead = -(-strip // 2 // 16) * 16

    half = ov_dev // 2
    packed = pack(intersections, width // 2)
    low, high = packed[:half], packed[half:]
    last_low, next_high = shift(low, 1), shift(high, -1)
    last_high, next_low = shift(high, 1), shift(low, -1)
    far_low, far_high = shift(last_low, 1), shift(next_high, -1)
    pieces = (packed, next_low, next_high, far_low, far_high, last_low, last_high)

    owner_row = lookup(pair_slot, coupling_list[0]) - group_index * coup
    reader_row = lookup(pair_slot, coupling_list[1])
    source, read_pair = reader_row // coup, reader_row % coup
    local_o = coupling_list[2] - group_index * (ov_dev * coup)
    local_o = (local_o - member * ov_dev) % (ov_dev * coup)
    position = lax.iota(jnp.int32, count)
    twin = jnp.max(
        jnp.where((source[None, :] == source[:, None]) & (position[None, :] < position[:, None]), 1, 0), axis=1
    )
    slot = 2 * source + twin
    chosen = slot[None, :] == position[:, None]
    pick = lambda v: jnp.sum(jnp.where(chosen, v[None, :], jnp.zeros((), v.dtype)), axis=1)
    strip_row = member * strip
    lane_tile = jnp.minimum(strip_row // 128, 2) * 128
    sched = jnp.concatenate(
        [pick(local_o), pick(owner_row), jnp.stack([strip_row - lane_tile, lane_tile, member])]
    ).astype(jnp.int32)
    weights = pick(coupling_weight)
    asked = source[None, :] == lax.broadcasted_iota(jnp.int32, (groups, count), 0)
    wanted = exchange_wanted(jnp.max(jnp.where(asked, read_pair[None, :], 0), axis=1))

    denominator = orbital_energy[:, :, None] + orbital_energy[:, None, :] + pair_energy[:, None, None]
    own_integrals = integrals.astype(jnp.float32)

    def to_strips(matrix):
        tiles = pack(jnp.transpose(matrix).reshape(coup, strip, width), lead)
        part = lambda d: lax.dynamic_index_in_dim(tiles, lax.rem(member + d, coup), keepdims=False)
        return jnp.stack([part(0)] + [shift(part(coup - e), coup - e) for e in range(1, coup)])

    rounded = to_strips((-own_integrals / denominator).astype(jnp.bfloat16)[0])
    integral_strips = to_strips(integrals[0])
    energies = jnp.concatenate([orbital_energy[0], pair_energy])[None]
    energies = jnp.concatenate([energies] + [shift(energies, -e) for e in range(1, coup)])
    orbital, pair = energies[:, :width], energies[:, width]
    own_rows = lax.dynamic_slice_in_dim(orbital, strip_row, strip, axis=1)
    strip_denominator = pack(own_rows[:, :, None] + orbital[:, None, :] + pair[:, None, None], lead)
    wanted = (wanted - member) % coup

    for iteration in range(ITERS):
        outgoing = rounded.at[wanted].get(mode="promise_in_bounds")
        arrived = lax.all_to_all(outgoing, PAIRS, 0, 0, tiled=True)
        arrived = pltpu.with_memory_space_constraint(arrived, pltpu.VMEM)
        last = iteration == ITERS - 1
        if iteration == 0:
            kept, *parts, table = couple(sched, weights, arrived, pieces, coup, strip, width, True)
        else:
            table = pltpu.with_memory_space_constraint(table, pltpu.VMEM)
            kept, *parts = couple(sched, weights, arrived, (table,), coup, strip, width, False)
        coupled = sum_parts(kept, parts)
        if not last:
            amplitudes = -(integral_strips.astype(jnp.float32) + coupled) / strip_denominator
            rounded = amplitudes.astype(jnp.bfloat16)
    return -(own_integrals + jnp.transpose(coupled)[None]) / denominator


def solution(mesh):
    split = Mesh(
        mesh.devices.reshape(4, 4, 2, mesh.shape["coup"]), ("pairs_0", "pairs_1", "pairs_2", "coup")
    )
    in_specs = (
        P(None, PAIRS),
        P(),
        P(PAIRS),
        P(PAIRS_COUP, None, None),
        P(PAIRS_COUP, None),
        P(PAIRS_COUP),
        P(PAIRS_COUP, None, None),
    )
    return jax.shard_map(
        amplitudes_of, mesh=split, in_specs=in_specs, out_specs=P(PAIRS_COUP, None, None), check_vma=False
    )
```

```python
import functools

import jax
import jax.numpy as jnp
from jax import lax
from jax.experimental import pallas as pl
from jax.experimental.pallas import tpu as pltpu
from jax.sharding import Mesh
from jax.sharding import PartitionSpec as P


ITERS = 2
PAIRS = ("pairs_0", "pairs_1", "pairs_2")
PAIRS_COUP = ("pairs_0", "pairs_1", "pairs_2", "coup")


def lookup(lookup_table, queries):
    columns = lax.broadcasted_iota(jnp.int32, (queries.shape[0], lookup_table.shape[0]), 1)
    return jnp.sum(jnp.where(queries[:, None] == columns, lookup_table[None, :], 0), axis=1)


def shift(x, step):
    peers = lax.axis_size("coup")
    return lax.ppermute(x, "coup", [(i, (i + step) % peers) for i in range(peers)])


def exchange_wanted(wanted_here):
    return lax.all_to_all(wanted_here[:, None, None], PAIRS, 0, 0, tiled=True)[:, 0, 0]


def pack(x, lead):
    whole = x.shape[-1] // 128 * 128
    tiles = [x[..., t : t + 128] for t in range(0, whole, 128)]
    tail = x[..., whole:]
    tiles.append(jnp.concatenate([tail[..., :lead, :], tail[..., -lead:, :]], axis=-1))
    return jnp.concatenate(tiles, axis=-2)


def halves(both):
    empty = jnp.zeros((both.shape[0], 64), both.dtype)
    return jnp.concatenate([both[:, :64], empty], axis=1), jnp.concatenate([both[:, 64:], empty], axis=1)


def start_table(pieces, o_buf, o_tail, sems):
    width, o_lead = o_buf.shape[1], o_tail.shape[1]
    full = width // 128
    copies, first = [], 0
    for piece in pieces:
        into = pl.ds(first, piece.shape[0])
        for t in range(full):
            copies.append((piece.at[:, pl.ds(t * width, width), :], o_buf.at[into, :, pl.ds(128 * t, 128)]))
        copies.append((piece.at[:, pl.ds(full * width, o_lead), :], o_tail.at[into]))
        first += piece.shape[0]
    copies = [pltpu.make_async_copy(src, dst, sems.at[i]) for i, (src, dst) in enumerate(copies)]
    for copy in copies:
        copy.start()
    return copies


def finish_table(copies, o_buf, o_tail):
    width, o_lead = o_buf.shape[1], o_tail.shape[1]
    for copy in copies:
        copy.wait()

    def unpack(i, carry):
        low, high = halves(o_tail[i])
        o_buf[i, 0:o_lead, width // 128 * 128 :] = low
        o_buf[i, width - o_lead :, width // 128 * 128 :] = high
        return carry

    lax.fori_loop(0, o_buf.shape[0], unpack, 0)


def couple_kernel(slices, unroll, sched, weights, t_ref, *refs):
    if slices:
        pieces, outs, table, refs = refs[:7], refs[7:11], refs[11], refs[12:]
        acc, t_tail, even_0, even_1, odd_0, odd_1, o_buf, sems, o_tail = refs
    else:
        table, outs, refs = refs[0], refs[1:5], refs[5:]
        acc, t_tail, even_0, even_1, odd_0, odd_1, o_buf, sems = refs
    sources, strip, width = t_tail.shape[0], t_tail.shape[1], o_buf.shape[1]
    full = width // 128
    t_lead = t_ref.shape[1] - full * strip
    count = 2 * sources
    offset = pl.multiple_of(sched[2 * count], 16)
    lane = pl.multiple_of(sched[2 * count + 1], 128)
    member = sched[2 * count + 2]
    if slices:
        copies = start_table(pieces, o_buf, o_tail, sems)
    else:
        copies = [pltpu.make_async_copy(table, o_buf, sems.at[0])]
        copies[0].start()
    for ref in (acc, even_0, even_1, odd_0, odd_1):
        ref[...] = jnp.zeros_like(ref)

    def unpack_t(h, carry):
        low, high = halves(t_ref[h, full * strip :, :])
        t_tail[h, 0:t_lead, :] = low
        t_tail[h, strip - t_lead :, :] = high
        return carry

    lax.fori_loop(0, sources, unpack_t, 0)
    if slices:
        finish_table(copies, o_buf, o_tail)
        written = pltpu.make_async_copy(o_buf, table, sems.at[0])
        written.start()
    else:
        copies[0].wait()

    def right(h, s, ref):
        tiles = [t_ref[h, strip * t : strip * t + strip, :] for t in range(full)] + [t_tail[h]]
        product = lax.dot_general(
            jnp.concatenate(tiles, axis=1), o_buf[sched[2 * h + s]], (((1,), (1,)), ((), ())),
            preferred_element_type=jnp.float32,
        )
        ref[pl.ds(offset, strip), :] = product.astype(jnp.bfloat16)

    def left(h, s, ref):
        k = 2 * h + s
        product = jnp.dot(
            o_buf[sched[k], :, pl.ds(lane, 256)], ref[...], preferred_element_type=jnp.float32
        )
        acc[sched[count + k]] += weights[k] * product

    right(0, 0, even_0)
    right(0, 1, even_1)

    def turn(i, carry):
        for u in range(unroll):
            h = 2 * (unroll * i + u)
            right(h + 1, 0, odd_0)
            left(h, 0, even_0)
            right(h + 1, 1, odd_1)
            left(h, 1, even_1)
            after = jnp.minimum(h + 2, sources - 1)
            right(after, 0, even_0)
            left(h + 1, 0, odd_0)
            right(after, 1, even_1)
            left(h + 1, 1, odd_1)
        return carry

    lax.fori_loop(0, sources // (2 * unroll), turn, 0)
    members = acc.shape[0]
    for d, out in enumerate(outs):
        peer = lax.rem(member + d, members)
        if slices:
            begin = pl.multiple_of(peer * strip, 16)
            for r in range(members):
                row = lax.rem(peer + r, members)
                for t in range(full):
                    part = acc[row, pl.ds(begin, strip), 128 * t : 128 * t + 128]
                    out[r, strip * t : strip * t + strip, :] = part.astype(out.dtype)
                tail = acc[row, pl.ds(begin, strip), 128 * full :]
                out[r, strip * full :, :] = jnp.concatenate(
                    [tail[:t_lead], tail[strip - t_lead :]], axis=1
                ).astype(out.dtype)
        else:
            out[...] = acc[peer].astype(out.dtype)
    if slices:
        written.wait()


def couple(sched, weights, strips, held, coup, strip, width, slices):
    sources, packed, _ = strips.shape
    full = width // 128
    total = sum(piece.shape[0] for piece in held)
    anywhere = pl.BlockSpec(memory_space=pl.ANY)
    part = (coup, packed, 128) if slices else (width, width)
    table = (total, width, 128 * full + 128)
    resident = pl.BlockSpec(memory_space=pltpu.VMEM)
    whole = pl.BlockSpec(part, lambda i, *_: (0,) * len(part))
    half = pltpu.VMEM((256, width), jnp.bfloat16)
    scratch = [
        pltpu.VMEM((coup, width, width), jnp.float32),
        pltpu.VMEM((sources, strip, 128), jnp.bfloat16),
        half, half, half, half,
    ]
    shapes = [jax.ShapeDtypeStruct(part, jnp.float32)] + [jax.ShapeDtypeStruct(part, jnp.bfloat16)] * 3
    scratch += [
        pltpu.VMEM(table, jnp.bfloat16),
        pltpu.SemaphoreType.DMA(((full + 1) * len(held),)),
    ]
    if slices:
        scratch.append(pltpu.VMEM((total, width // 2, 128), jnp.bfloat16))
        shapes.append(pltpu.HBM(table, jnp.bfloat16))
    return pl.pallas_call(
        functools.partial(couple_kernel, slices, 4),
        out_shape=shapes,
        grid_spec=pltpu.PrefetchScalarGridSpec(
            num_scalar_prefetch=2,
            grid=(1,),
            in_specs=[resident] + [anywhere] * len(held),
            out_specs=[whole] * 4 + ([pl.BlockSpec(memory_space=pltpu.HBM)] if slices else []),
            scratch_shapes=scratch,
        ),
        compiler_params=pltpu.CompilerParams(vmem_limit_bytes=32 * 2**20),
        name="couple_strips" if slices else "couple_pairs",
    )(sched, weights, strips, *held)


def sum_parts(kept, parts):
    for d, part in enumerate(parts):
        moved = shift(part, d + 1)
        kept = kept + moved.astype(jnp.float32)
    return kept


def amplitudes_of(
    coupling_list, pair_slot, coupling_weight, integrals, orbital_energy, pair_energy, intersections
):
    groups = lax.axis_size(PAIRS)
    coup = lax.axis_size("coup")
    group_index = lax.axis_index(PAIRS)
    member = lax.axis_index("coup")
    ov_dev, width = intersections.shape[0], integrals.shape[-1]
    count = coupling_list.shape[1]
    strip = width // coup
    lead = -(-strip // 2 // 16) * 16

    half = ov_dev // 2
    packed = pack(intersections, width // 2)
    low, high = packed[:half], packed[half:]
    last_low, next_high = shift(low, 1), shift(high, -1)
    last_high, next_low = shift(high, 1), shift(low, -1)
    far_low, far_high = shift(last_low, 1), shift(next_high, -1)
    pieces = (packed, next_low, next_high, far_low, far_high, last_low, last_high)

    owner_row = lookup(pair_slot, coupling_list[0]) - group_index * coup
    reader_row = lookup(pair_slot, coupling_list[1])
    source, read_pair = reader_row // coup, reader_row % coup
    local_o = coupling_list[2] - group_index * (ov_dev * coup)
    local_o = (local_o - member * ov_dev) % (ov_dev * coup)
    position = lax.iota(jnp.int32, count)
    twin = jnp.max(
        jnp.where((source[None, :] == source[:, None]) & (position[None, :] < position[:, None]), 1, 0), axis=1
    )
    slot = 2 * source + twin
    chosen = slot[None, :] == position[:, None]
    pick = lambda v: jnp.sum(jnp.where(chosen, v[None, :], jnp.zeros((), v.dtype)), axis=1)
    strip_row = member * strip
    lane_tile = jnp.minimum(strip_row // 128, 2) * 128
    sched = jnp.concatenate(
        [pick(local_o), pick(owner_row), jnp.stack([strip_row - lane_tile, lane_tile, member])]
    ).astype(jnp.int32)
    weights = pick(coupling_weight)
    asked = source[None, :] == lax.broadcasted_iota(jnp.int32, (groups, count), 0)
    wanted = exchange_wanted(jnp.max(jnp.where(asked, read_pair[None, :], 0), axis=1))

    denominator = orbital_energy[:, :, None] + orbital_energy[:, None, :] + pair_energy[:, None, None]
    own_integrals = integrals.astype(jnp.float32)

    def to_strips(matrix):
        tiles = pack(jnp.transpose(matrix).reshape(coup, strip, width), lead)
        part = lambda d: lax.dynamic_index_in_dim(tiles, lax.rem(member + d, coup), keepdims=False)
        return jnp.stack([part(0)] + [shift(part(coup - e), coup - e) for e in range(1, coup)])

    rounded = to_strips((-own_integrals / denominator).astype(jnp.bfloat16)[0])
    integral_strips = to_strips(integrals[0])
    energies = jnp.concatenate([orbital_energy[0], pair_energy])[None]
    energies = jnp.concatenate([energies] + [shift(energies, -e) for e in range(1, coup)])
    orbital, pair = energies[:, :width], energies[:, width]
    own_rows = lax.dynamic_slice_in_dim(orbital, strip_row, strip, axis=1)
    strip_denominator = pack(own_rows[:, :, None] + orbital[:, None, :] + pair[:, None, None], lead)
    wanted = (wanted - member) % coup

    for iteration in range(ITERS):
        outgoing = rounded.at[wanted].get(mode="promise_in_bounds")
        arrived = lax.all_to_all(outgoing, PAIRS, 0, 0, tiled=True)
        arrived = pltpu.with_memory_space_constraint(arrived, pltpu.VMEM)
        last = iteration == ITERS - 1
        if iteration == 0:
            kept, *parts, table = couple(sched, weights, arrived, pieces, coup, strip, width, True)
        else:
            table = pltpu.with_memory_space_constraint(table, pltpu.HBM)
            kept, *parts = couple(sched, weights, arrived, (table,), coup, strip, width, False)
        coupled = sum_parts(kept, parts)
        if not last:
            amplitudes = -(integral_strips.astype(jnp.float32) + coupled) / strip_denominator
            rounded = amplitudes.astype(jnp.bfloat16)
    return -(own_integrals + jnp.transpose(coupled)[None]) / denominator


def solution(mesh):
    split = Mesh(
        mesh.devices.reshape(4, 4, 2, mesh.shape["coup"]), ("pairs_0", "pairs_1", "pairs_2", "coup")
    )
    in_specs = (
        P(None, PAIRS),
        P(),
        P(PAIRS),
        P(PAIRS_COUP, None, None),
        P(PAIRS_COUP, None),
        P(PAIRS_COUP),
        P(PAIRS_COUP, None, None),
    )
    return jax.shard_map(
        amplitudes_of, mesh=split, in_specs=in_specs, out_specs=P(PAIRS_COUP, None, None), check_vma=False
    )
```
